512 devices in a mesh: grp: 16 (over z), voc: 32 (over x, y, core).
Axes of the slice: x: 4, y: 4, z: 16, core: 2. Of those that a mesh axis runs over, the one named last changes fastest.
Arguments:
- hidden_states: bfloat16 [16384, 8192], P('grp', 'voc'), may hold values from -6 to 6
- target_logits: float32 [16384, 16384], P('grp', 'voc'), may hold values from -12 to 240
- labels: int32 [16384, 8], P('grp'), may hold values from 0 to 2047
- down_weight: bfloat16 [8192, 256], P('voc'), may hold values from -0.0625 to 0.0625
- up_weight: bfloat16 [256, 8192], P(None, 'grp'), may hold values from -0.75 to 0.75
- head_weight: bfloat16 [8192, 16384], P('grp', 'voc'), may hold values from -0.0625 to 0.0625
Outputs:
- frame_loss: float32 [32, 16, 256], P('voc', 'grp')
- grad_a: float32 [8192, 256], P('voc')
- grad_b: float32 [256, 8192], P(None, 'grp')
The draws below stay inside these ranges and needn't reach their ends.
All inputs are finite; a program needn't handle non-finite values.
Results may differ from the reference program's by a relative error of at most 0.0046.
Values may be sent and summed in bfloat16 or wider, within the bound.
A program may use at most 64 MiB of HBM per device.

```python
import math
import jax
import jax.numpy as jnp
import numpy as np
from jax import lax

D = 8192
CODEBOOKS = 8
CB = 2048
R = 256
HEAD = 2
F = 1024
V = 16384
Q = 4
FB = 256
FRAMES = 16384
N_GRP = 16


def draw_target_logits(key, part):
    subkeys = jax.random.split(key, 1)
    full_shape = (FRAMES, CODEBOOKS, CB)
    values = jnp.clip(jax.random.normal(subkeys[0], full_shape, jnp.float32) * 3.0, -12.0, 12.0)
    return values.reshape(FRAMES, CODEBOOKS * CB)


def touch_ends(values, stream_key, smallest, top_value):
    index_at = [jax.random.randint(jax.random.fold_in(stream_key, axis), (), 0, length) for axis, length in enumerate(values.shape)]
    longest = values.shape.index(max(values.shape))
    next_to = index_at[:longest] + [(index_at[longest] + 1) % values.shape[longest]] + index_at[longest + 1:]
    return values.at[tuple(index_at)].set(smallest).at[tuple(next_to)].set(top_value)


def shard_levels(key, extent, shards, least, top_value):
    loudness = 1.0
    for dim, parts in shards:
        draws = jax.random.uniform(jax.random.fold_in(jax.random.fold_in(key, 6), dim), (parts,), jnp.float32, least / len(shards), top_value / len(shards))
        loudness = loudness * jnp.repeat(jnp.exp(draws), extent[dim] // parts).reshape((-1,) + (1,) * (len(extent) - 1 - dim))
    return loudness


def rank_table(count, slope):
    portions = [(1 << 20) // math.isqrt(standing ** slope) + 1 for standing in range(1, count + 1)]
    deviation = 1 + sum(portions) // (1 << 30)
    return np.cumsum(np.array([max(1, weight // deviation) for weight in portions]))


def ranked_ids(rng, dims, number_of, slope):
    table = rank_table(number_of, slope)
    lot = jax.random.randint(jax.random.fold_in(rng, 1), dims, 0, int(table[number_of - 1]))
    grade = jnp.searchsorted(jnp.asarray(table, jnp.int32), lot, side="right")
    return jax.random.permutation(jax.random.fold_in(rng, 2), number_of)[grade].astype(jnp.int32)


def scatter_about(stream_key, dims, scale, limit, shards=(), kind=jnp.bfloat16):
    values = jax.random.normal(stream_key, dims, jnp.float32) * scale
    if len(shards) > 0:
        values = shard_levels(stream_key, dims, shards, -0.22, 0.18) * values
    return jnp.clip(values, min=-limit, max=limit).astype(kind)


def setup_inputs(seed: int = 0) -> dict:
    streams_of = jax.random.split(jax.random.key(seed), 7)
    return {
        "hidden_states": scatter_about(streams_of[0], (FRAMES, D), 1.0, 6.0, ((0, 16), (1, 32))),
        "target_logits": draw_target_logits(jax.random.fold_in(streams_of[6], 71), 0),
        "labels": touch_ends(ranked_ids(streams_of[2], (FRAMES, CODEBOOKS), CB, 2), jax.random.fold_in(streams_of[2], 3), 0, CB - 1).astype(jnp.int32),
        "down_weight": scatter_about(streams_of[3], (D, R), D ** -0.5, 0.0625, ((0, 32),)),
        "up_weight": scatter_about(streams_of[4], (R, D), (R // 4) ** -0.5, 0.75, ((1, 16),)),
        "head_weight": scatter_about(streams_of[5], (D, V), D ** -0.5, 0.0625, ((0, 16), (1, 32))),
    }


LAM = 0.1


def silu_slope(values):
    sigma = jax.nn.sigmoid(values)
    return sigma * (1.0 + values * (1.0 - sigma))


def reference(hidden_states, target_logits, labels, down_weight, up_weight, head_weight):
    pre_act = jnp.dot(hidden_states, down_weight, preferred_element_type=jnp.float32)
    activation = jax.nn.silu(pre_act).astype(jnp.bfloat16)
    vocab_proj = jnp.dot(up_weight, head_weight, preferred_element_type=jnp.float32).astype(jnp.bfloat16)
    shifted = jnp.concatenate([target_logits[HEAD:], jnp.zeros((HEAD, V), jnp.float32)], 0)
    live_mask = (jnp.arange(FRAMES) < FRAMES - HEAD).astype(jnp.float32)
    scanned = (target_logits.reshape(N_GRP, F, V), shifted.reshape(N_GRP, F, V),
               activation.reshape(N_GRP, F, R), labels.reshape(N_GRP, F, CODEBOOKS),
               live_mask.reshape(N_GRP, F))

    def group_step(accumulated, pieces):
        target_rows, shifted_rows, act_rows, label_rows, live_rows = pieces
        draft_logits = (target_rows.astype(jnp.float32)
                        + jnp.dot(act_rows, vocab_proj, preferred_element_type=jnp.float32))
        log_target = jax.nn.log_softmax(shifted_rows.astype(jnp.float32).reshape(F, CODEBOOKS, CB), -1)
        log_draft = jax.nn.log_softmax(draft_logits.reshape(F, CODEBOOKS, CB), -1)
        target_prob = jnp.exp(log_target)
        draft_prob = jnp.exp(log_draft)
        onehot = (jnp.arange(CB)[None, None, :] == label_rows[:, :, None]).astype(jnp.float32)
        divergence = jnp.sum(target_prob * (log_target - log_draft), -1)
        picked = jnp.sum(onehot * log_draft, -1)
        frame_rows = live_rows[:, None] * divergence - LAM * picked
        logit_grad = (live_rows[:, None, None] * (draft_prob - target_prob)
                      + LAM * (draft_prob - onehot)).astype(jnp.bfloat16).reshape(F, V)
        accumulated = accumulated + lax.dot_general(act_rows, logit_grad, (((0,), (0,)), ((), ())),
                                                    preferred_element_type=jnp.float32)
        act_grad = jnp.dot(logit_grad, vocab_proj.T, preferred_element_type=jnp.float32)
        return accumulated, (frame_rows, act_grad)

    proj_grad, (frame_rows, act_grad) = lax.scan(group_step, jnp.zeros((R, V), jnp.float32), scanned)
    act_grad = act_grad.reshape(FRAMES, R)
    pre_grad = (act_grad * silu_slope(pre_act)).astype(jnp.bfloat16)
    grad_a = jnp.dot(hidden_states.T, pre_grad, preferred_element_type=jnp.float32)
    grad_b = jnp.dot(proj_grad.astype(jnp.bfloat16), head_weight.T, preferred_element_type=jnp.float32)
    frame_loss = frame_rows.reshape(N_GRP, Q, FB, CODEBOOKS).transpose(3, 1, 0, 2).reshape(CODEBOOKS * Q, N_GRP, FB)
    return frame_loss, grad_a, grad_b
```

```python
import functools

import jax
import jax.numpy as jnp
from jax import lax
from jax.experimental import pallas as pl
from jax.experimental.pallas import tpu as pltpu
from jax.sharding import PartitionSpec as P

HEAD = 2
LAM = 0.1
MESH = pl.DeviceIdType.MESH
F32 = jnp.float32
BF16 = jnp.bfloat16
CHUNK = 128
WIRE = {"a": F32, "v": BF16, "b": F32, "p": BF16, "g": F32, "ag": F32, "c": F32, "ac": F32}

PHASES = (
    "halo", "pair_a", "rs_a", "ag_a", "back_a", "s1", "s2", "s3",
    "pair_b", "rs_b", "ag_b", "back_b", "pair_c", "rs_c", "ag_c", "back_c",
) + tuple(
    ring + stage
    for ring in ("v", "p", "g")
    for stage in ("_up", "_down", "_near", "_ahead", "_behind", "_rest")
)
HOP = 4
SEM = {name: number for number, name in enumerate(PHASES)}


def dot_nt(left, right):
    return lax.dot_general(left, right, (((1,), (1,)), ((), ())), preferred_element_type=F32)


def dot_nn(left, right):
    return jnp.dot(left, right, preferred_element_type=F32)


def kernel(
    n_grp, n_voc, n_book,
    h_any, t_any, lab_ref, dw_any, uw_any, hw_any,
    loss_ref, ga_ref, gb_ref,
    h, t, dw, uw, hw, h_t,
    pv, pv_s, pv_o, pv_r, vp,
    pa, pair_a, pa2, rv_a, pre, acts, acts_t,
    labc, ssh, et, ed, statcol, stat, rv_s, comb, grad,
    pp, pp_s, pp_o, pp_r, proj,
    pb, pair_b, pb2, rv_b, pg,
    px, px_s, px_o, px_r, gag,
    pc, pair_c, pc2, rv_c, gcol, gpart,
    in_sem, send_sem, recv_sem,
):
    g = lax.axis_index("grp")
    v = lax.axis_index("voc")
    chips = n_voc // 2
    chip = v // 2
    core = v % 2
    other = 1 - core
    twin = chip * 2 + other
    per_book = n_voc // n_book
    book = v // per_book
    part = v % per_book
    rows, width = ssh.shape
    rank = vp.shape[0]
    half = rows // 2
    a_rows = half // chips
    v_rows = rank // n_grp
    c_rows = rank // chips
    half_w = gb_ref.shape[1] // 2

    loads = [
        pltpu.make_async_copy(uw_any, uw, in_sem.at[0]),
        pltpu.make_async_copy(hw_any, hw, in_sem.at[1]),
        pltpu.make_async_copy(h_any, h, in_sem.at[2]),
        pltpu.make_async_copy(dw_any, dw, in_sem.at[3]),
        pltpu.make_async_copy(t_any, t.at[pl.ds(0, rows)], in_sem.at[4]),
    ]
    for load in loads:
        load.start()

    def z_peer(offset):
        return {"grp": lax.rem(g + offset, n_grp), "voc": v}

    def chip_peer(offset):
        return {"grp": g, "voc": lax.rem(chip + offset, chips) * 2 + core}

    def book_peer(offset):
        return {"grp": g, "voc": book * per_book + lax.rem(part + offset, per_book)}

    barrier = pltpu.get_barrier_semaphore()

    def greet(device):
        pl.semaphore_signal(barrier, inc=1, device_id=device, device_id_type=MESH)

    def loop(count, body):
        def step(index, carry):
            body(index)
            return carry
        lax.fori_loop(0, count, step, 0)

    for hop in range(1, HOP + 1):
        greet(z_peer(hop))
        greet(z_peer(n_grp - hop))
    loop(chips - 1, lambda i: greet(chip_peer(i + 1)))
    greet({"grp": g, "voc": twin})
    greet({"grp": g, "voc": book * per_book + lax.rem(part + 2, per_book) // 2 * 2 + other})

    def remote(src, dst, name, device):
        return pltpu.make_async_remote_copy(
            src_ref=src, dst_ref=dst, send_sem=send_sem.at[SEM[name]],
            recv_sem=recv_sem.at[SEM[name]], device_id=device, device_id_type=MESH,
        )

    def wait_for(ref, name):
        pltpu.make_async_copy(ref, ref, recv_sem.at[SEM[name]]).wait()

    def wait_sent(ref, name):
        pltpu.make_async_copy(ref, ref, send_sem.at[SEM[name]]).wait()

    def ordered(index, count):
        return count // 2 + jnp.where(index % 2 == 0, -(index // 2), (index + 1) // 2)

    def scatter(src, piece, dst, name, peer, me, count):
        def send(index):
            offset = ordered(index, count)
            target = lax.rem(me + offset, count)
            remote(
                src.at[pl.ds(pl.multiple_of(target * piece, piece), piece)],
                dst.at[offset - 1], name, peer(offset),
            ).start()
        loop(count - 1, send)

    def gather(ref, piece, start, name, peer, count):
        def send(index):
            offset = ordered(index, count)
            mine = ref.at[pl.ds(pl.multiple_of(start, piece), piece)]
            remote(mine, mine, name, peer(offset)).start()
        loop(count - 1, send)

    def total(own, ref, count):
        acc = own
        for slot in range(count - 1):
            acc = acc + ref[slot].astype(F32)
        return acc

    def block_of(ref, distance, piece):
        where = lax.rem(g + n_grp + distance, n_grp)
        return ref.at[pl.ds(pl.multiple_of(where * piece, piece), piece)]

    def ring_peer(distance):
        return z_peer(n_grp + distance)

    def ring_scatter(name, src, slots, piece):
        for hop in range(HOP, 0, -1):
            remote(
                block_of(src, hop + HOP, piece), slots.at[hop - 1], name + "_up", ring_peer(hop)
            ).start()
            if hop < HOP:
                remote(
                    block_of(src, -hop - HOP, piece), slots.at[HOP + hop - 1], name + "_down",
                    ring_peer(-hop),
                ).start()
        for hop in range(HOP - 1, 0, -1):
            for way in (1, -1):
                slot = slots.at[2 * HOP - 1 + hop - 1 + (0 if way > 0 else HOP - 1)]
                remote(
                    block_of(src, way * hop, piece), slot, name + "_near", ring_peer(way * hop)
                ).start()

    def ring_relay(name, raw, out, slots, piece):
        first = 4 * HOP - 3
        for way, tag, low, count in ((1, "_up", 0, HOP), (-1, "_down", HOP, HOP - 1)):
            wait_for(slots.at[pl.ds(low, count)], name + tag)
            acc = block_of(raw, way * HOP, piece)[...]
            for slot in range(low, low + count):
                acc = acc + slots[slot].astype(F32)
            side = 0 if way > 0 else 1
            out[side] = acc.astype(out.dtype)
            remote(out.at[side], slots.at[first + side], name + "_near", ring_peer(way * HOP)).start()

    def ring_total(name, raw, slots, piece):
        low, count = 2 * HOP - 1, 2 * HOP
        wait_for(slots.at[pl.ds(low, count)], name + "_near")
        acc = block_of(raw, 0, piece)[...]
        for slot in range(low, low + count):
            acc = acc + slots[slot].astype(F32)
        return acc

    def ring_gather(name, ref, piece):
        mine = block_of(ref, 0, piece)
        for hop in range(HOP, 0, -1):
            for way, tag in ((1, "_ahead"), (-1, "_behind")):
                kind = tag if hop == HOP else "_rest"
                remote(mine, mine, name + kind, ring_peer(way * hop)).start()

    def ring_forward(name, ref, piece):
        for way, tag, last in ((1, "_ahead", HOP), (-1, "_behind", HOP - 1)):
            held = block_of(ref, -way * HOP, piece)
            wait_for(held, name + tag)
            for hop in range(last, 0, -1):
                remote(held, held, name + "_rest", ring_peer(way * hop)).start()

    def ring_done(name, ref, piece):
        wait_for(ref.at[pl.ds(0, (n_grp - 3) * piece)], name + "_rest")

    def ring_sent(name, slots, ref, piece):
        wait_sent(slots.at[pl.ds(0, HOP)], name + "_up")
        wait_sent(slots.at[pl.ds(0, HOP - 1)], name + "_down")
        wait_sent(slots.at[pl.ds(0, 2 * HOP)], name + "_near")
        wait_sent(ref.at[pl.ds(0, piece)], name + "_ahead")
        wait_sent(ref.at[pl.ds(0, piece)], name + "_behind")
        wait_sent(ref.at[pl.ds(0, (n_grp - 3) * piece)], name + "_rest")

    def turn(src, dst):
        def body(index):
            at = pl.ds(pl.multiple_of(index * 256, 256), 256)
            dst[:, at] = src[at, :].T
        loop(rows // 256, body)

    loads[0].wait()
    loads[1].wait()
    pv[...] = dot_nn(uw[...], hw[...])
    pv_s[...] = pv[...].astype(pv_s.dtype)
    pl.semaphore_wait(barrier, 2 * HOP + chips - 1 + 2)
    ring_scatter("v", pv_s, pv_r, v_rows)
    remote(
        t_any.at[pl.ds(0, 8)], t.at[pl.ds(rows, 8)], "halo", ring_peer(-1)
    ).start()
    loads[2].wait()
    loads[3].wait()

    def first(index):
        at = pl.ds(pl.multiple_of(index * 256, 256), 256)
        value = dot_nn(h[at, :], dw[...])
        pa[at, :] = value
    loop(rows // 256, first)

    mine_half = pl.ds(pl.multiple_of(core * half, half), half)
    twin_half = pl.ds(pl.multiple_of(other * half, half), half)
    twin_id = {"grp": g, "voc": twin}
    remote(pa.at[twin_half], pair_a, "pair_a", twin_id).start()
    wait_for(pair_a, "pair_a")
    pa2[...] = (pa[mine_half, :] + pair_a[...]).astype(pa2.dtype)
    scatter(pa2, a_rows, rv_a, "rs_a", chip_peer, chip, chips)

    turn(h, h_t)
    loads[4].wait()
    ring_relay("v", pv, pv_o, pv_r, v_rows)
    wait_for(t.at[pl.ds(rows, 8)], "halo")
    t[pl.ds(rows, 8), :] = jnp.where(g == n_grp - 1, 0.0, t[pl.ds(rows, 8), :])

    def target_pass(index):
        start = pl.multiple_of(index * CHUNK, CHUNK)
        at = pl.ds(start, CHUNK)
        block = t[pl.ds(start, CHUNK + 8), :]
        shifted = pltpu.roll(block, CHUNK + 8 - HEAD, 0)[:CHUNK]
        top = jnp.max(shifted, -1, keepdims=True)
        low = shifted - top
        expo = jnp.exp(low)
        ssh[at, :] = low
        et[at, :] = expo
        norm = jnp.sum(expo, -1, keepdims=True)
        lane = lax.broadcasted_iota(jnp.int32, (CHUNK, 128), 1)
        statcol[at, :] = jnp.where(lane == 0, top, jnp.where(lane == 1, norm, 0.0))
        ids = lab_ref[at, :].astype(F32)
        which = lax.broadcasted_iota(jnp.int32, ids.shape, 1)
        label = jnp.sum(jnp.where(which == book, ids, 0.0), -1, keepdims=True)
        labc[at, :] = jnp.broadcast_to(label - (part * width).astype(F32), (CHUNK, 128))
    loop(rows // CHUNK, target_pass)
    comb[...] = jnp.zeros_like(comb)

    ring_own = pl.ds(pl.multiple_of(g * v_rows, v_rows), v_rows)
    vp[ring_own, :] = ring_total("v", pv, pv_r, v_rows).astype(BF16)
    ring_gather("v", vp, v_rows)

    a_start = chip * a_rows
    own_a = pl.ds(pl.multiple_of(a_start, a_rows), a_rows)
    wait_for(rv_a, "rs_a")
    pre_own = total(pa2[own_a, :].astype(F32), rv_a, chips)
    pre[...] = pre_own
    acts_at = core * half + a_start
    acts[pl.ds(pl.multiple_of(acts_at, a_rows), a_rows), :] = (
        pre_own / (1.0 + jnp.exp(-pre_own))
    ).astype(BF16)
    gather(acts, a_rows, acts_at, "ag_a", chip_peer, chips)
    ring_forward("v", vp, v_rows)

    wait_for(acts.at[pl.ds(0, (chips - 1) * a_rows)], "ag_a")
    remote(acts.at[mine_half], acts.at[mine_half], "back_a", twin_id).start()

    wait_for(acts.at[twin_half], "back_a")
    turn(acts, acts_t)
    ring_done("v", vp, v_rows)

    def label_mask(at):
        labels = labc[at, :]
        col = lax.broadcasted_iota(jnp.int32, (CHUNK, 128), 1).astype(F32)
        return jnp.concatenate([labels == col + 128.0 * k for k in range(width // 128)], 1)

    def draft_pass(index):
        start = pl.multiple_of(index * CHUNK, CHUNK)
        at = pl.ds(start, CHUNK)
        draft = t[at, :] + dot_nn(acts[at, :], vp[...])
        top = jnp.max(draft, -1, keepdims=True)
        low = draft - top
        expo = jnp.exp(low)
        ed[at, :] = expo
        norm = jnp.sum(expo, -1, keepdims=True)
        cross = jnp.sum(et[at, :] * (ssh[at, :] - low), -1, keepdims=True)
        picked = jnp.sum(jnp.where(label_mask(at), draft, 0.0), -1, keepdims=True)
        lane = lax.broadcasted_iota(jnp.int32, (CHUNK, 128), 1)
        cols = statcol[at, :]
        cols = jnp.where(lane == 2, top, cols)
        cols = jnp.where(lane == 3, norm, cols)
        cols = jnp.where(lane == 4, cross, cols)
        cols = jnp.where(lane == 5, picked, cols)
        stat[:, at] = cols.T[:8]
    loop(rows // CHUNK, draft_pass)

    for offset in range(1, per_book):
        remote(stat, rv_s.at[offset - 1], f"s{offset}", book_peer(offset)).start()
    for offset in range(1, per_book):
        wait_for(rv_s.at[offset - 1], f"s{offset}")

    blocks = [stat[...]] + [rv_s[k] for k in range(per_book - 1)]

    def row(block, k):
        return block[k:k + 1, :]

    top_t = functools.reduce(jnp.maximum, [row(b, 0) for b in blocks])
    top_d = functools.reduce(jnp.maximum, [row(b, 2) for b in blocks])
    fac_t = [jnp.exp(row(b, 0) - top_t) for b in blocks]
    fac_d = [jnp.exp(row(b, 2) - top_d) for b in blocks]
    sum_t = sum(row(b, 1) * f for b, f in zip(blocks, fac_t))
    sum_d = sum(row(b, 3) * f for b, f in zip(blocks, fac_d))
    cross = sum(
        f * (row(b, 4) + row(b, 1) * ((row(b, 0) - top_t) - (row(b, 2) - top_d)))
        for b, f in zip(blocks, fac_t)
    )
    picked = sum(row(b, 5) for b in blocks) - top_d - jnp.log(sum_d)
    frame = g * rows + lax.broadcasted_iota(jnp.int32, (1, rows), 1)
    live = (frame < rows * n_grp - HEAD).astype(F32)
    diverge = cross / sum_t - jnp.log(sum_t) + jnp.log(sum_d)
    comb[0:1, :] = (live + LAM) * fac_d[0] / sum_d
    comb[1:2, :] = live * fac_t[0] / sum_t
    comb[2:3, :] = live * diverge - LAM * picked
    block_rows = rows // per_book
    loss_ref[0] = comb[2:3, pl.ds(pl.multiple_of(part * block_rows, block_rows), block_rows)]

    def grad_pass(index):
        at = pl.ds(pl.multiple_of(index * CHUNK, CHUNK), CHUNK)
        cols = comb[:, at].T
        value = ed[at, :] * cols[:, 0:1] - et[at, :] * cols[:, 1:2]
        value = value - jnp.where(label_mask(at), LAM, 0.0)
        grad[at, :] = value.astype(BF16)
    loop(rows // CHUNK, grad_pass)

    pp[...] = dot_nn(acts_t[...], grad[...])
    pp_s[...] = pp[...].astype(pp_s.dtype)
    ring_scatter("p", pp_s, pp_r, v_rows)

    def back(index):
        at = pl.ds(pl.multiple_of(index * 256, 256), 256)
        value = dot_nt(grad[at, :], vp[...])
        pb[at, :] = value
    loop(rows // 256, back)
    remote(pb.at[twin_half], pair_b, "pair_b", twin_id).start()
    wait_for(pair_b, "pair_b")
    pb2[...] = (pb[mine_half, :] + pair_b[...]).astype(pb2.dtype)
    scatter(pb2, a_rows, rv_b, "rs_b", chip_peer, chip, chips)
    ring_relay("p", pp, pp_o, pp_r, v_rows)
    proj[ring_own, :] = ring_total("p", pp, pp_r, v_rows).astype(BF16)
    ring_gather("p", proj, v_rows)
    wait_for(rv_b, "rs_b")
    act_grad = total(pb2[own_a, :].astype(F32), rv_b, chips)
    sigma = 1.0 / (1.0 + jnp.exp(-pre[...]))
    slope = sigma * (1.0 + pre[...] * (1.0 - sigma))
    pg[pl.ds(pl.multiple_of(acts_at, a_rows), a_rows), :] = (act_grad * slope).astype(BF16)
    gather(pg, a_rows, acts_at, "ag_b", chip_peer, chips)

    ring_forward("p", proj, v_rows)

    wait_for(pg.at[pl.ds(0, (chips - 1) * a_rows)], "ag_b")
    remote(pg.at[mine_half], pg.at[mine_half], "back_b", twin_id).start()
    wait_for(pg.at[twin_half], "back_b")
    px[...] = dot_nn(h_t[...], pg[...])
    px_s[...] = px[...].astype(px_s.dtype)
    ring_scatter("g", px_s, px_r, v_rows)

    ring_done("p", proj, v_rows)
    up = dot_nt(proj[...], hw[...])
    for side in range(2):
        pc[side] = up[:, side * half_w:(side + 1) * half_w]
    remote(pc.at[other], pair_c, "pair_c", twin_id).start()
    wait_for(pair_c, "pair_c")
    pc2[...] = (pc[core] + pair_c[...]).astype(pc2.dtype)
    scatter(pc2, c_rows, rv_c, "rs_c", chip_peer, chip, chips)

    ring_relay("g", px, px_o, px_r, v_rows)
    gag[ring_own, :] = ring_total("g", px, px_r, v_rows).astype(gag.dtype)
    ring_gather("g", gag, v_rows)

    own_c = pl.ds(pl.multiple_of(chip * c_rows, c_rows), c_rows)
    wait_for(rv_c, "rs_c")
    gcol[own_c, :] = total(pc2[own_c, :].astype(F32), rv_c, chips).astype(gcol.dtype)
    gather(gcol, c_rows, chip * c_rows, "ag_c", chip_peer, chips)
    ring_forward("g", gag, v_rows)
    wait_for(gcol.at[pl.ds(0, (chips - 1) * c_rows)], "ag_c")
    remote(gcol, gpart, "back_c", twin_id).start()

    ring_done("g", gag, v_rows)
    ga_ref[...] = gag[...].astype(F32)
    wait_for(gpart, "back_c")

    mine = gcol[...].astype(F32)
    theirs = gpart[...].astype(F32)
    gb_ref[:, :half_w] = jnp.where(core == 0, mine, theirs)
    gb_ref[:, half_w:] = jnp.where(core == 0, theirs, mine)

    wait_sent(t.at[pl.ds(rows, 8)], "halo")
    wait_sent(pair_a, "pair_a")
    wait_sent(rv_a, "rs_a")
    wait_sent(acts.at[pl.ds(0, (chips - 1) * a_rows)], "ag_a")
    wait_sent(acts.at[mine_half], "back_a")
    ring_sent("v", pv_r, vp, v_rows)
    for offset in range(1, per_book):
        wait_sent(stat, f"s{offset}")
    wait_sent(pair_b, "pair_b")
    wait_sent(rv_b, "rs_b")
    wait_sent(pg.at[pl.ds(0, (chips - 1) * a_rows)], "ag_b")
    wait_sent(pg.at[mine_half], "back_b")
    ring_sent("p", pp_r, proj, v_rows)
    ring_sent("g", px_r, gag, v_rows)
    wait_sent(pair_c, "pair_c")
    wait_sent(rv_c, "rs_c")
    wait_sent(gcol.at[pl.ds(0, (chips - 1) * c_rows)], "ag_c")
    wait_sent(gcol, "back_c")


def on_device(n_grp, n_voc, hidden_states, target_logits, labels, down_weight, up_weight, head_weight):
    rows, width = target_logits.shape
    n_book = labels.shape[1]
    per_book = n_voc // n_book
    deep = hidden_states.shape[1]
    rank = up_weight.shape[0]
    span = up_weight.shape[1]
    chips = n_voc // 2
    half = rows // 2
    a_rows = half // chips
    v_rows = rank // n_grp
    c_rows = rank // chips
    half_w = span // 2
    vm = pltpu.VMEM
    w = WIRE
    scratch = [
        vm((rows, deep), BF16), vm((rows + 8, width), F32), vm((deep, rank), BF16),
        vm((rank, span), BF16), vm((span, width), BF16), vm((deep, rows), BF16),
        vm((rank, width), F32), vm((rank, width), w["v"]), vm((2, v_rows, width), w["v"]),
        vm((4 * HOP - 1, v_rows, width), w["v"]), vm((rank, width), BF16),
        vm((rows, rank), F32), vm((half, rank), F32),
        vm((half, rank), w["a"]), vm((chips - 1, a_rows, rank), w["a"]), vm((a_rows, rank), F32),
        vm((rows, rank), BF16), vm((rank, rows), BF16),
        vm((rows, 128), F32), vm((rows, width), F32), vm((rows, width), F32),
        vm((rows, width), F32), vm((rows, 128), F32), vm((8, rows), F32),
        vm((per_book - 1, 8, rows), F32), vm((128, rows), F32), vm((rows, width), BF16),
        vm((rank, width), F32), vm((rank, width), w["p"]), vm((2, v_rows, width), w["p"]),
        vm((4 * HOP - 1, v_rows, width), w["p"]), vm((rank, width), BF16),
        vm((rows, rank), F32), vm((half, rank), F32),
        vm((half, rank), w["b"]), vm((chips - 1, a_rows, rank), w["b"]), vm((rows, rank), BF16),
        vm((deep, rank), F32), vm((deep, rank), w["g"]), vm((2, v_rows, rank), w["g"]),
        vm((4 * HOP - 1, v_rows, rank), w["g"]), vm((deep, rank), w["ag"]),
        vm((2, rank, half_w), F32), vm((rank, half_w), F32),
        vm((rank, half_w), w["c"]), vm((chips - 1, c_rows, half_w), w["c"]), vm((rank, half_w), w["ac"]),
        vm((rank, half_w), w["ac"]),
        pltpu.SemaphoreType.DMA((5,)),
        pltpu.SemaphoreType.DMA((len(PHASES),)),
        pltpu.SemaphoreType.DMA((len(PHASES),)),
    ]
    hbm = pl.BlockSpec(memory_space=pl.ANY)
    vmem = pl.BlockSpec(memory_space=pltpu.VMEM)
    return pl.pallas_call(
        functools.partial(kernel, n_grp, n_voc, n_book),
        out_shape=(
            jax.ShapeDtypeStruct((1, 1, rows // per_book), F32),
            jax.ShapeDtypeStruct((deep, rank), F32),
            jax.ShapeDtypeStruct((rank, span), F32),
        ),
        in_specs=[hbm, hbm, vmem, hbm, hbm, hbm],
        out_specs=(vmem, vmem, vmem),
        scratch_shapes=scratch,
        compiler_params=pltpu.CompilerParams(
            collective_id=0, has_side_effects=True, vmem_limit_bytes=60 * 1024 * 1024
        ),
    )(hidden_states, target_logits, labels, down_weight, up_weight, head_weight)


def solution(mesh):
    in_specs = (
        P("grp", "voc"),
        P("grp", "voc"),
        P("grp", None),
        P("voc", None),
        P(None, "grp"),
        P("grp", "voc"),
    )
    out_specs = (P("voc", "grp", None), P("voc", None), P(None, "grp"))
    return jax.shard_map(
        functools.partial(on_device, mesh.shape["grp"], mesh.shape["voc"]),
        mesh=mesh, in_specs=in_specs, out_specs=out_specs, check_vma=False,
    )
```

```python
import functools

import jax
import jax.numpy as jnp
from jax import lax
from jax.experimental import pallas as pl
from jax.experimental.pallas import tpu as pltpu
from jax.sharding import PartitionSpec as P

HEAD = 2
LAM = 0.1
MESH = pl.DeviceIdType.MESH
F32 = jnp.float32
BF16 = jnp.bfloat16
CHUNK = 128
WIRE = {
    "a": F32, "b": F32, "c": BF16, "v": BF16, "vn": BF16, "vx": F32,
    "p": BF16, "pn": BF16, "px": BF16, "g": BF16, "gn": BF16, "gx": BF16, "ga": F32,
}

PHASES = (
    "halo", "pair_a", "rs_a", "ag_a", "back_a", "s1", "s2", "s3",
    "pair_b", "rs_b", "ag_b", "back_b", "rs_c", "ag_c",
) + tuple(
    ring + stage
    for ring in ("v", "p", "g")
    for stage in ("_up", "_down", "_near", "_far", "_ahead", "_behind", "_rest")
)
HOP = 4
SEM = {name: number for number, name in enumerate(PHASES)}


def dot_nt(left, right):
    return lax.dot_general(left, right, (((1,), (1,)), ((), ())), preferred_element_type=F32)


def dot_nn(left, right):
    return jnp.dot(left, right, preferred_element_type=F32)


def kernel(
    n_grp, n_voc, n_book,
    h_any, t_any, lab_any, dw_any, uw_any, hw_any,
    loss_ref, ga_ref, gb_ref,
    h, t, lab, dw, uw, hw, h_t,
    pv, pv_s, pv_o, pv_f, pv_n, pv_r, vp,
    pa, pair_a, pa2, rv_a, pre, acts, acts_t,
    labc, ssh, et, ed, statcol, stat, rv_s, comb, grad,
    pp, pp_s, pp_o, pp_f, pp_n, pp_r, proj,
    pb, pair_b, pb2, rv_b, pg,
    px, px_s, px_o, px_f, px_n, px_r, gag,
    pc, pc_s, rv_c, gall,
    in_sem, send_sem, recv_sem,
):
    g = lax.axis_index("grp")
    v = lax.axis_index("voc")
    chips = n_voc // 2
    chip = v // 2
    core = v % 2
    other = 1 - core
    twin = chip * 2 + other
    per_book = n_voc // n_book
    book = v // per_book
    part = v % per_book
    rows, width = ssh.shape
    rank = vp.shape[0]
    half = rows // 2
    a_rows = half // chips
    v_rows = rank // n_grp
    c_rows = rank // chips
    half_w = gb_ref.shape[2]

    loads = [
        pltpu.make_async_copy(uw_any, uw, in_sem.at[0]),
        pltpu.make_async_copy(hw_any, hw, in_sem.at[1]),
        pltpu.make_async_copy(h_any, h, in_sem.at[2]),
        pltpu.make_async_copy(dw_any, dw, in_sem.at[3]),
        pltpu.make_async_copy(t_any, t.at[pl.ds(0, rows)], in_sem.at[4]),
        pltpu.make_async_copy(lab_any, lab, in_sem.at[5]),
    ]
    for load in loads:
        load.start()

    def z_peer(offset):
        return {"grp": lax.rem(g + offset, n_grp), "voc": v}

    def chip_peer(offset):
        return {"grp": g, "voc": lax.rem(chip + offset, chips) * 2 + core}

    def voc_peer(offset):
        return {"grp": g, "voc": lax.rem(v + offset, n_voc)}

    def book_peer(offset):
        return {"grp": g, "voc": book * per_book + lax.rem(part + offset, per_book)}

    barrier = pltpu.get_barrier_semaphore()

    def greet(device):
        pl.semaphore_signal(barrier, inc=1, device_id=device, device_id_type=MESH)

    def loop(count, body):
        def step(index, carry):
            body(index)
            return carry
        lax.fori_loop(0, count, step, 0)

    for hop in range(1, HOP + 1):
        greet(z_peer(hop))
        greet(z_peer(n_grp - hop))
    loop(n_voc - 1, lambda i: greet(voc_peer(i + 1)))

    def remote(src, dst, name, device):
        return pltpu.make_async_remote_copy(
            src_ref=src, dst_ref=dst, send_sem=send_sem.at[SEM[name]],
            recv_sem=recv_sem.at[SEM[name]], device_id=device, device_id_type=MESH,
        )

    def wait_for(ref, name):
        pltpu.make_async_copy(ref, ref, recv_sem.at[SEM[name]]).wait()

    def wait_sent(ref, name):
        pltpu.make_async_copy(ref, ref, send_sem.at[SEM[name]]).wait()

    def ordered(index, count):
        return count // 2 + jnp.where(index % 2 == 0, -(index // 2), (index + 1) // 2)

    def scatter(src, piece, dst, name, peer, me, count):
        def send(index):
            offset = ordered(index, count)
            target = lax.rem(me + offset, count)
            remote(
                src.at[pl.ds(pl.multiple_of(target * piece, piece), piece)],
                dst.at[offset - 1], name, peer(offset),
            ).start()
        loop(count - 1, send)

    def gather(ref, piece, start, name, peer, count):
        def send(index):
            offset = ordered(index, count)
            mine = ref.at[pl.ds(pl.multiple_of(start, piece), piece)]
            remote(mine, mine, name, peer(offset)).start()
        loop(count - 1, send)

    def total(own, ref, count):
        acc = own
        for slot in range(count - 1):
            acc = acc + ref[slot].astype(F32)
        return acc

    def block_of(ref, distance, piece):
        where = lax.rem(g + n_grp + distance, n_grp)
        return ref.at[pl.ds(pl.multiple_of(where * piece, piece), piece)]

    def ring_peer(distance):
        return z_peer(n_grp + distance)

    def ring_scatter(name, raw, src, slots, near, piece):
        for hop in range(HOP, 0, -1):
            remote(
                block_of(src, hop + HOP, piece), slots.at[hop - 1], name + "_up", ring_peer(hop)
            ).start()
            if hop < HOP:
                remote(
                    block_of(src, -hop - HOP, piece), slots.at[HOP + hop - 1], name + "_down",
                    ring_peer(-hop),
                ).start()
        for hop in range(HOP - 1, 0, -1):
            for way in (1, -1):
                slot = near.at[hop - 1 + (0 if way > 0 else HOP - 1)]
                origin = raw if near.dtype == raw.dtype else src
                remote(
                    block_of(origin, way * hop, piece), slot, name + "_near", ring_peer(way * hop)
                ).start()

    def ring_relay(name, raw, out, far, slots, piece):
        for way, tag, low, count in ((1, "_up", 0, HOP), (-1, "_down", HOP, HOP - 1)):
            wait_for(slots.at[pl.ds(low, count)], name + tag)
            acc = block_of(raw, way * HOP, piece)[...]
            for slot in range(low, low + count):
                acc = acc + slots[slot].astype(F32)
            side = 0 if way > 0 else 1
            out[side] = acc.astype(out.dtype)
            remote(out.at[side], far.at[side], name + "_far", ring_peer(way * HOP)).start()

    def ring_total(name, raw, far, near, piece):
        wait_for(near, name + "_near")
        acc = block_of(raw, 0, piece)[...]
        for slot in range(2 * HOP - 2):
            acc = acc + near[slot].astype(F32)
        wait_for(far, name + "_far")
        return acc + far[0].astype(F32) + far[1].astype(F32)

    def ring_gather(name, ref, piece):
        mine = block_of(ref, 0, piece)
        for hop in range(HOP, 0, -1):
            for way, tag in ((1, "_ahead"), (-1, "_behind")):
                kind = tag if hop == HOP else "_rest"
                remote(mine, mine, name + kind, ring_peer(way * hop)).start()

    def ring_forward(name, ref, piece):
        for way, tag, last in ((1, "_ahead", HOP), (-1, "_behind", HOP - 1)):
            held = block_of(ref, -way * HOP, piece)
            wait_for(held, name + tag)
            for hop in range(last, 0, -1):
                remote(held, held, name + "_rest", ring_peer(way * hop)).start()

    def ring_done(name, ref, piece):
        wait_for(ref.at[pl.ds(0, (n_grp - 3) * piece)], name + "_rest")

    def ring_sent(name, far, slots, near, ref, piece):
        wait_sent(slots.at[pl.ds(0, HOP)], name + "_up")
        wait_sent(slots.at[pl.ds(0, HOP - 1)], name + "_down")
        wait_sent(near, name + "_near")
        wait_sent(far, name + "_far")
        wait_sent(ref.at[pl.ds(0, piece)], name + "_ahead")
        wait_sent(ref.at[pl.ds(0, piece)], name + "_behind")
        wait_sent(ref.at[pl.ds(0, (n_grp - 3) * piece)], name + "_rest")

    def turn(src, dst):
        def body(index):
            at = pl.ds(pl.multiple_of(index * 256, 256), 256)
            dst[:, at] = src[at, :].T
        loop(rows // 256, body)

    loads[0].wait()
    loads[1].wait()
    pv[...] = dot_nn(uw[...], hw[...])
    pv_s[...] = pv[...].astype(pv_s.dtype)
    pl.semaphore_wait(barrier, 2 * HOP + n_voc - 1)
    ring_scatter("v", pv, pv_s, pv_r, pv_n, v_rows)
    remote(
        t_any.at[pl.ds(0, 8)], t.at[pl.ds(rows, 8)], "halo", ring_peer(-1)
    ).start()
    loads[2].wait()
    loads[3].wait()

    mine_half = pl.ds(pl.multiple_of(core * half, half), half)
    twin_half = pl.ds(pl.multiple_of(other * half, half), half)
    twin_id = {"grp": g, "voc": twin}

    def half_dots(dst, start, left, dot, right):
        def body(index):
            at = pl.ds(pl.multiple_of(start + index * 256, 256), 256)
            dst[at, :] = dot(left[at, :], right[...])
        loop(half // 256, body)

    half_dots(pa, other * half, h, dot_nn, dw)

    remote(pa.at[twin_half], pair_a, "pair_a", twin_id).start()
    half_dots(pa, core * half, h, dot_nn, dw)
    wait_for(pair_a, "pair_a")
    pa2[...] = (pa[mine_half, :] + pair_a[...]).astype(pa2.dtype)
    scatter(pa2, a_rows, rv_a, "rs_a", chip_peer, chip, chips)

    turn(h, h_t)
    loads[4].wait()
    loads[5].wait()
    ring_relay("v", pv, pv_o, pv_f, pv_r, v_rows)
    wait_for(t.at[pl.ds(rows, 8)], "halo")
    t[pl.ds(rows, 8), :] = jnp.where(g == n_grp - 1, 0.0, t[pl.ds(rows, 8), :])

    def target_pass(index):
        start = pl.multiple_of(index * CHUNK, CHUNK)
        at = pl.ds(start, CHUNK)
        block = t[pl.ds(start, CHUNK + 8), :]
        shifted = pltpu.roll(block, CHUNK + 8 - HEAD, 0)[:CHUNK]
        top = jnp.max(shifted, -1, keepdims=True)
        low = shifted - top
        expo = jnp.exp(low)
        ssh[at, :] = low
        et[at, :] = expo
        norm = jnp.sum(expo, -1, keepdims=True)
        lane = lax.broadcasted_iota(jnp.int32, (CHUNK, 128), 1)
        statcol[at, :] = jnp.where(lane == 0, top, jnp.where(lane == 1, norm, 0.0))
        ids = lab[:, at].astype(F32)
        which = lax.broadcasted_iota(jnp.int32, ids.shape, 0)
        label = jnp.sum(jnp.where(which == book, ids, 0.0), 0, keepdims=True)
        label = label - (part * width).astype(F32)
        labc[at, :] = jnp.broadcast_to(label, (CHUNK, CHUNK)).T
    loop(rows // CHUNK, target_pass)
    comb[...] = jnp.zeros_like(comb)

    ring_own = pl.ds(pl.multiple_of(g * v_rows, v_rows), v_rows)
    vp[ring_own, :] = ring_total("v", pv, pv_f, pv_n, v_rows).astype(BF16)
    ring_gather("v", vp, v_rows)

    a_start = chip * a_rows
    own_a = pl.ds(pl.multiple_of(a_start, a_rows), a_rows)
    wait_for(rv_a, "rs_a")
    pre_own = total(pa2[own_a, :].astype(F32), rv_a, chips)
    pre[...] = pre_own
    acts_at = core * half + a_start
    acts[pl.ds(pl.multiple_of(acts_at, a_rows), a_rows), :] = (
        pre_own / (1.0 + jnp.exp(-pre_own))
    ).astype(BF16)
    gather(acts, a_rows, acts_at, "ag_a", chip_peer, chips)
    ring_forward("v", vp, v_rows)

    wait_for(acts.at[pl.ds(0, (chips - 1) * a_rows)], "ag_a")
    remote(acts.at[mine_half], acts.at[mine_half], "back_a", twin_id).start()

    ring_done("v", vp, v_rows)

    def label_mask(at):
        labels = labc[at, :]
        col = lax.broadcasted_iota(jnp.int32, (CHUNK, 128), 1).astype(F32)
        return jnp.concatenate([labels == col + 128.0 * k for k in range(width // 128)], 1)

    def draft_pass(index):
        start = pl.multiple_of(index * CHUNK, CHUNK)
        at = pl.ds(start, CHUNK)
        draft = t[at, :] + dot_nn(acts[at, :], vp[...])
        top = jnp.max(draft, -1, keepdims=True)
        low = draft - top
        expo = jnp.exp(low)
        ed[at, :] = expo
        norm = jnp.sum(expo, -1, keepdims=True)
        cross = jnp.sum(et[at, :] * (ssh[at, :] - low), -1, keepdims=True)
        picked = jnp.sum(jnp.where(label_mask(at), draft, 0.0), -1, keepdims=True)
        lane = lax.broadcasted_iota(jnp.int32, (CHUNK, 128), 1)
        cols = statcol[at, :]
        cols = jnp.where(lane == 2, top, cols)
        cols = jnp.where(lane == 3, norm, cols)
        cols = jnp.where(lane == 4, cross, cols)
        cols = jnp.where(lane == 5, picked, cols)
        stat[:, at] = cols.T[:8]
    steps = half // CHUNK
    loop(steps, lambda index: draft_pass(core * steps + index))
    wait_for(acts.at[twin_half], "back_a")
    loop(steps, lambda index: draft_pass(other * steps + index))

    for offset in range(1, per_book):
        remote(stat, rv_s.at[offset - 1], f"s{offset}", book_peer(offset)).start()
    turn(acts, acts_t)
    for offset in range(1, per_book):
        wait_for(rv_s.at[offset - 1], f"s{offset}")

    blocks = [stat[...]] + [rv_s[k] for k in range(per_book - 1)]

    def row(block, k):
        return block[k:k + 1, :]

    top_t = functools.reduce(jnp.maximum, [row(b, 0) for b in blocks])
    top_d = functools.reduce(jnp.maximum, [row(b, 2) for b in blocks])
    fac_t = [jnp.exp(row(b, 0) - top_t) for b in blocks]
    fac_d = [jnp.exp(row(b, 2) - top_d) for b in blocks]
    sum_t = sum(row(b, 1) * f for b, f in zip(blocks, fac_t))
    sum_d = sum(row(b, 3) * f for b, f in zip(blocks, fac_d))
    cross = sum(
        f * (row(b, 4) + row(b, 1) * ((row(b, 0) - top_t) - (row(b, 2) - top_d)))
        for b, f in zip(blocks, fac_t)
    )
    picked = sum(row(b, 5) for b in blocks) - top_d - jnp.log(sum_d)
    frame = g * rows + lax.broadcasted_iota(jnp.int32, (1, rows), 1)
    live = (frame < rows * n_grp - HEAD).astype(F32)
    diverge = cross / sum_t - jnp.log(sum_t) + jnp.log(sum_d)
    comb[0:1, :] = (live + LAM) * fac_d[0] / sum_d
    comb[1:2, :] = live * fac_t[0] / sum_t
    comb[2:3, :] = live * diverge - LAM * picked
    block_rows = rows // per_book
    loss_ref[0] = comb[2:3, pl.ds(pl.multiple_of(part * block_rows, block_rows), block_rows)]

    def grad_pass(index):
        at = pl.ds(pl.multiple_of(index * CHUNK, CHUNK), CHUNK)
        cols = comb[:, at].T
        value = ed[at, :] * cols[:, 0:1] - et[at, :] * cols[:, 1:2]
        value = value - jnp.where(label_mask(at), LAM, 0.0)
        grad[at, :] = value.astype(BF16)
    loop(rows // CHUNK, grad_pass)

    pp[...] = dot_nn(acts_t[...], grad[...])
    pp_s[...] = pp[...].astype(pp_s.dtype)
    ring_scatter("p", pp, pp_s, pp_r, pp_n, v_rows)

    half_dots(pb, other * half, grad, dot_nt, vp)
    remote(pb.at[twin_half], pair_b, "pair_b", twin_id).start()
    half_dots(pb, core * half, grad, dot_nt, vp)
    wait_for(pair_b, "pair_b")
    pb2[...] = (pb[mine_half, :] + pair_b[...]).astype(pb2.dtype)
    scatter(pb2, a_rows, rv_b, "rs_b", chip_peer, chip, chips)
    ring_relay("p", pp, pp_o, pp_f, pp_r, v_rows)
    wait_for(rv_b, "rs_b")
    act_grad = total(pb2[own_a, :].astype(F32), rv_b, chips)
    sigma = 1.0 / (1.0 + jnp.exp(-pre[...]))
    slope = sigma * (1.0 + pre[...] * (1.0 - sigma))
    pg[pl.ds(pl.multiple_of(acts_at, a_rows), a_rows), :] = (act_grad * slope).astype(BF16)
    gather(pg, a_rows, acts_at, "ag_b", chip_peer, chips)

    proj[ring_own, :] = ring_total("p", pp, pp_f, pp_n, v_rows).astype(BF16)
    ring_gather("p", proj, v_rows)
    ring_forward("p", proj, v_rows)

    wait_for(pg.at[pl.ds(0, (chips - 1) * a_rows)], "ag_b")
    remote(pg.at[mine_half], pg.at[mine_half], "back_b", twin_id).start()
    wait_for(pg.at[twin_half], "back_b")
    px[...] = dot_nn(h_t[...], pg[...])
    px_s[...] = px[...].astype(px_s.dtype)
    ring_scatter("g", px, px_s, px_r, px_n, v_rows)

    ring_done("p", proj, v_rows)
    up = dot_nt(proj[...], hw[...])
    for side in range(2):
        pc[side] = up[:, side * half_w:(side + 1) * half_w]
        pc_s[side] = up[:, side * half_w:(side + 1) * half_w].astype(pc_s.dtype)

    def c_block(ref, device):
        return ref.at[device % 2, pl.ds(pl.multiple_of(device // 2 * c_rows, c_rows), c_rows)]

    def send_c(index):
        offset = ordered(index, n_voc)
        target = lax.rem(v + offset, n_voc)
        remote(c_block(pc_s, target), rv_c.at[offset - 1], "rs_c", voc_peer(offset)).start()
    loop(n_voc - 1, send_c)

    ring_relay("g", px, px_o, px_f, px_r, v_rows)
    gag[ring_own, :] = ring_total("g", px, px_f, px_n, v_rows).astype(gag.dtype)
    ring_gather("g", gag, v_rows)

    wait_for(rv_c, "rs_c")
    c_block(gall, v)[...] = total(c_block(pc, v)[...], rv_c, n_voc).astype(gall.dtype)

    def share_c(index):
        block = c_block(gall, v)
        remote(block, block, "ag_c", voc_peer(ordered(index, n_voc))).start()
    loop(n_voc - 1, share_c)
    ring_forward("g", gag, v_rows)
    ring_done("g", gag, v_rows)
    ga_ref[...] = gag[...]
    wait_for(rv_c, "ag_c")
    gb_ref[...] = gall[...]

    wait_sent(t.at[pl.ds(rows, 8)], "halo")
    wait_sent(pair_a, "pair_a")
    wait_sent(rv_a, "rs_a")
    wait_sent(acts.at[pl.ds(0, (chips - 1) * a_rows)], "ag_a")
    wait_sent(acts.at[mine_half], "back_a")
    ring_sent("v", pv_f, pv_r, pv_n, vp, v_rows)
    for offset in range(1, per_book):
        wait_sent(stat, f"s{offset}")
    wait_sent(pair_b, "pair_b")
    wait_sent(rv_b, "rs_b")
    wait_sent(pg.at[pl.ds(0, (chips - 1) * a_rows)], "ag_b")
    wait_sent(pg.at[mine_half], "back_b")
    ring_sent("p", pp_f, pp_r, pp_n, proj, v_rows)
    ring_sent("g", px_f, px_r, px_n, gag, v_rows)
    wait_sent(rv_c, "rs_c")
    wait_sent(rv_c, "ag_c")


def finish(loss_ref, ga_ref, gb_ref, loss_out, ga_out, gb_out):
    half_w = gb_ref.shape[2]
    loss_out[...] = loss_ref[...]
    ga_out[...] = ga_ref[...].astype(F32)
    for side in range(2):
        gb_out[:, side * half_w:(side + 1) * half_w] = gb_ref[side].astype(F32)


def on_device(n_grp, n_voc, hidden_states, target_logits, labels, down_weight, up_weight, head_weight):
    rows, width = target_logits.shape
    n_book = labels.shape[1]
    per_book = n_voc // n_book
    deep = hidden_states.shape[1]
    rank = up_weight.shape[0]
    span = up_weight.shape[1]
    chips = n_voc // 2
    half = rows // 2
    a_rows = half // chips
    v_rows = rank // n_grp
    c_rows = rank // chips
    half_w = span // 2
    vm = pltpu.VMEM
    w = WIRE
    scratch = [
        vm((rows, deep), BF16), vm((rows + 8, width), F32), vm((n_book, rows), jnp.int32), vm((deep, rank), BF16),
        vm((rank, span), BF16), vm((span, width), BF16), vm((deep, rows), BF16),
        vm((rank, width), F32), vm((rank, width), w["v"]), vm((2, v_rows, width), w["vx"]),
        vm((2, v_rows, width), w["vx"]), vm((2 * HOP - 2, v_rows, width), w["vn"]),
        vm((2 * HOP - 1, v_rows, width), w["v"]), vm((rank, width), BF16),
        vm((rows, rank), F32), vm((half, rank), F32),
        vm((half, rank), w["a"]), vm((chips - 1, a_rows, rank), w["a"]), vm((a_rows, rank), F32),
        vm((rows, rank), BF16), vm((rank, rows), BF16),
        vm((rows, 128), F32), vm((rows, width), F32), vm((rows, width), F32),
        vm((rows, width), F32), vm((rows, 128), F32), vm((8, rows), F32),
        vm((per_book - 1, 8, rows), F32), vm((128, rows), F32), vm((rows, width), BF16),
        vm((rank, width), F32), vm((rank, width), w["p"]), vm((2, v_rows, width), w["px"]),
        vm((2, v_rows, width), w["px"]), vm((2 * HOP - 2, v_rows, width), w["pn"]),
        vm((2 * HOP - 1, v_rows, width), w["p"]), vm((rank, width), BF16),
        vm((rows, rank), F32), vm((half, rank), F32),
        vm((half, rank), w["b"]), vm((chips - 1, a_rows, rank), w["b"]), vm((rows, rank), BF16),
        vm((deep, rank), F32), vm((deep, rank), w["g"]), vm((2, v_rows, rank), w["gx"]),
        vm((2, v_rows, rank), w["gx"]), vm((2 * HOP - 2, v_rows, rank), w["gn"]),
        vm((2 * HOP - 1, v_rows, rank), w["g"]), vm((deep, rank), w["ga"]),
        vm((2, rank, half_w), F32), vm((2, rank, half_w), w["c"]),
        vm((n_voc - 1, c_rows, half_w), w["c"]), vm((2, rank, half_w), w["c"]),
        pltpu.SemaphoreType.DMA((6,)),
        pltpu.SemaphoreType.DMA((len(PHASES),)),
        pltpu.SemaphoreType.DMA((len(PHASES),)),
    ]
    hbm = pl.BlockSpec(memory_space=pl.ANY)
    vmem = pl.BlockSpec(memory_space=pltpu.VMEM)
    parts = pl.pallas_call(
        functools.partial(kernel, n_grp, n_voc, n_book),
        out_shape=(
            jax.ShapeDtypeStruct((1, 1, rows // per_book), F32),
            jax.ShapeDtypeStruct((deep, rank), w["ga"]),
            jax.ShapeDtypeStruct((2, rank, half_w), w["c"]),
        ),
        in_specs=[hbm] * 6,
        out_specs=(vmem, vmem, vmem),
        scratch_shapes=scratch,
        compiler_params=pltpu.CompilerParams(
            collective_id=0, has_side_effects=True, vmem_limit_bytes=56 * 1024 * 1024
        ),
    )(hidden_states, target_logits, labels.T, down_weight, up_weight, head_weight)
    return pl.pallas_call(
        finish,
        out_shape=(
            jax.ShapeDtypeStruct((1, 1, rows // per_book), F32),
            jax.ShapeDtypeStruct((deep, rank), F32),
            jax.ShapeDtypeStruct((rank, span), F32),
        ),
        in_specs=[vmem] * 3,
        out_specs=(vmem, vmem, vmem),
    )(*parts)


def solution(mesh):
    in_specs = (
        P("grp", "voc"),
        P("grp", "voc"),
        P("grp", None),
        P("voc", None),
        P(None, "grp"),
        P("grp", "voc"),
    )
    out_specs = (P("voc", "grp", None), P("voc", None), P(None, "grp"))
    return jax.shard_map(
        functools.partial(on_device, mesh.shape["grp"], mesh.shape["voc"]),
        mesh=mesh, in_specs=in_specs, out_specs=out_specs, check_vma=False,
    )
```

```python
import functools

import jax
import jax.numpy as jnp
from jax import lax
from jax.experimental import pallas as pl
from jax.experimental.pallas import tpu as pltpu
from jax.sharding import PartitionSpec as P

HEAD = 2
LAM = 0.1
MESH = pl.DeviceIdType.MESH
F32 = jnp.float32
BF16 = jnp.bfloat16
CHUNK = 128
WIRE = {
    "a": F32, "b": F32, "c": BF16, "v": BF16, "vn": BF16, "vx": F32,
    "p": BF16, "pn": BF16, "px": BF16, "g": BF16, "gn": BF16, "gx": BF16, "ga": BF16,
}

PHASES = (
    "halo", "pair_a", "rs_a", "ag_a", "back_a", "s01", "s02", "s03", "s11", "s12", "s13",
    "pair_b", "rs_b", "ag_b", "back_b", "rs_c", "ag_c",
) + tuple(
    ring + stage
    for ring in ("v", "p", "g")
    for stage in ("_up", "_down", "_near", "_far", "_ahead", "_behind", "_rest")
)
HOP = 4
SEM = {name: number for number, name in enumerate(PHASES)}


def dot_nt(left, right):
    return lax.dot_general(left, right, (((1,), (1,)), ((), ())), preferred_element_type=F32)


def dot_nn(left, right):
    return jnp.dot(left, right, preferred_element_type=F32)


def kernel(
    n_grp, n_voc, n_book,
    h_any, t_any, lab_any, dw_any, uw_any, hw_any,
    loss_ref, ga_ref, gb_ref,
    h, t, lab, dw, uw, hw, h_t,
    pv, pv_s, pv_o, pv_f, pv_n, pv_r, vp,
    pa, pair_a, pa2, rv_a, pre, acts, acts_t,
    labc, ssh, et, ed, statcol, stat, rv_s, comb, grad,
    pp, pp_s, pp_o, pp_f, pp_n, pp_r, proj,
    pb, pair_b, pb2, rv_b, pg,
    px, px_s, px_o, px_f, px_n, px_r, gag,
    pc, pc_s, rv_c, gall,
    in_sem, send_sem, recv_sem,
):
    g = lax.axis_index("grp")
    v = lax.axis_index("voc")
    chips = n_voc // 2
    chip = v // 2
    core = v % 2
    other = 1 - core
    twin = chip * 2 + other
    per_book = n_voc // n_book
    book = v // per_book
    part = v % per_book
    rows, width = ssh.shape
    rank = vp.shape[0]
    half = rows // 2
    a_rows = half // chips
    v_rows = rank // n_grp
    c_rows = rank // chips
    half_w = gb_ref.shape[2]

    loads = [
        pltpu.make_async_copy(uw_any, uw, in_sem.at[0]),
        pltpu.make_async_copy(hw_any, hw, in_sem.at[1]),
        pltpu.make_async_copy(h_any, h, in_sem.at[2]),
        pltpu.make_async_copy(dw_any, dw, in_sem.at[3]),
        pltpu.make_async_copy(t_any, t.at[pl.ds(0, rows)], in_sem.at[4]),
        pltpu.make_async_copy(lab_any, lab, in_sem.at[5]),
    ]
    for load in loads:
        load.start()

    def z_peer(offset):
        return {"grp": lax.rem(g + offset, n_grp), "voc": v}

    def chip_peer(offset):
        return {"grp": g, "voc": lax.rem(chip + offset, chips) * 2 + core}

    def voc_peer(offset):
        return {"grp": g, "voc": lax.rem(v + offset, n_voc)}

    def book_peer(offset):
        return {"grp": g, "voc": book * per_book + lax.rem(part + offset, per_book)}

    barrier = pltpu.get_barrier_semaphore()

    def greet(device):
        pl.semaphore_signal(barrier, inc=1, device_id=device, device_id_type=MESH)

    def loop(count, body):
        def step(index, carry):
            body(index)
            return carry
        lax.fori_loop(0, count, step, 0)

    for hop in range(1, HOP + 1):
        greet(z_peer(hop))
        greet(z_peer(n_grp - hop))
    loop(n_voc - 1, lambda i: greet(voc_peer(i + 1)))

    def remote(src, dst, name, device):
        return pltpu.make_async_remote_copy(
            src_ref=src, dst_ref=dst, send_sem=send_sem.at[SEM[name]],
            recv_sem=recv_sem.at[SEM[name]], device_id=device, device_id_type=MESH,
        )

    def wait_for(ref, name):
        pltpu.make_async_copy(ref, ref, recv_sem.at[SEM[name]]).wait()

    def wait_sent(ref, name):
        pltpu.make_async_copy(ref, ref, send_sem.at[SEM[name]]).wait()

    def ordered(index, count):
        return count // 2 + jnp.where(index % 2 == 0, -(index // 2), (index + 1) // 2)

    def scatter(src, piece, dst, name, peer, me, count):
        def send(index):
            offset = ordered(index, count)
            target = lax.rem(me + offset, count)
            remote(
                src.at[pl.ds(pl.multiple_of(target * piece, piece), piece)],
                dst.at[offset - 1], name, peer(offset),
            ).start()
        loop(count - 1, send)

    def gather(ref, piece, start, name, peer, count):
        def send(index):
            offset = ordered(index, count)
            mine = ref.at[pl.ds(pl.multiple_of(start, piece), piece)]
            remote(mine, mine, name, peer(offset)).start()
        loop(count - 1, send)

    def total(own, ref, count):
        acc = own
        for slot in range(count - 1):
            acc = acc + ref[slot].astype(F32)
        return acc

    def block_of(ref, distance, piece):
        where = lax.rem(g + n_grp + distance, n_grp)
        return ref.at[pl.ds(pl.multiple_of(where * piece, piece), piece)]

    def ring_peer(distance):
        return z_peer(n_grp + distance)

    def ring_scatter(name, raw, src, slots, near, piece):
        for hop in range(HOP, 0, -1):
            remote(
                block_of(src, hop + HOP, piece), slots.at[hop - 1], name + "_up", ring_peer(hop)
            ).start()
            if hop < HOP:
                remote(
                    block_of(src, -hop - HOP, piece), slots.at[HOP + hop - 1], name + "_down",
                    ring_peer(-hop),
                ).start()
        for hop in range(HOP - 1, 0, -1):
            for way in (1, -1):
                slot = near.at[hop - 1 + (0 if way > 0 else HOP - 1)]
                origin = raw if near.dtype == raw.dtype else src
                remote(
                    block_of(origin, way * hop, piece), slot, name + "_near", ring_peer(way * hop)
                ).start()

    def ring_relay(name, raw, out, far, slots, piece):
        for way, tag, low, count in ((1, "_up", 0, HOP), (-1, "_down", HOP, HOP - 1)):
            wait_for(slots.at[pl.ds(low, count)], name + tag)
            acc = block_of(raw, way * HOP, piece)[...]
            for slot in range(low, low + count):
                acc = acc + slots[slot].astype(F32)
            side = 0 if way > 0 else 1
            out[side] = acc.astype(out.dtype)
            remote(out.at[side], far.at[side], name + "_far", ring_peer(way * HOP)).start()

    def ring_total(name, raw, far, near, piece):
        wait_for(near, name + "_near")
        acc = block_of(raw, 0, piece)[...]
        for slot in range(2 * HOP - 2):
            acc = acc + near[slot].astype(F32)
        wait_for(far, name + "_far")
        return acc + far[0].astype(F32) + far[1].astype(F32)

    def ring_gather(name, ref, piece):
        mine = block_of(ref, 0, piece)
        for hop in range(HOP, 0, -1):
            for way, tag in ((1, "_ahead"), (-1, "_behind")):
                kind = tag if hop == HOP else "_rest"
                remote(mine, mine, name + kind, ring_peer(way * hop)).start()

    def ring_forward(name, ref, piece):
        for way, tag, last in ((1, "_ahead", HOP), (-1, "_behind", HOP - 1)):
            held = block_of(ref, -way * HOP, piece)
            wait_for(held, name + tag)
            for hop in range(last, 0, -1):
                remote(held, held, name + "_rest", ring_peer(way * hop)).start()

    def ring_done(name, ref, piece):
        wait_for(ref.at[pl.ds(0, (n_grp - 3) * piece)], name + "_rest")

    def ring_sent(name, far, slots, near, ref, piece):
        wait_sent(slots.at[pl.ds(0, HOP)], name + "_up")
        wait_sent(slots.at[pl.ds(0, HOP - 1)], name + "_down")
        wait_sent(near, name + "_near")
        wait_sent(far, name + "_far")
        wait_sent(ref.at[pl.ds(0, piece)], name + "_ahead")
        wait_sent(ref.at[pl.ds(0, piece)], name + "_behind")
        wait_sent(ref.at[pl.ds(0, (n_grp - 3) * piece)], name + "_rest")

    def turn(src, dst):
        def body(index):
            at = pl.ds(pl.multiple_of(index * 256, 256), 256)
            dst[:, at] = src[at, :].T
        loop(rows // 256, body)

    loads[0].wait()
    loads[1].wait()
    pv[...] = dot_nn(uw[...], hw[...])
    pv_s[...] = pv[...].astype(pv_s.dtype)
    loads[2].wait()
    loads[3].wait()

    mine_half = pl.ds(pl.multiple_of(core * half, half), half)
    twin_half = pl.ds(pl.multiple_of(other * half, half), half)
    twin_id = {"grp": g, "voc": twin}

    def half_dots(dst, start, left, dot, right):
        def body(index):
            at = pl.ds(pl.multiple_of(start + index * 256, 256), 256)
            dst[at, :] = dot(left[at, :], right[...])
        loop(half // 256, body)

    half_dots(pa, other * half, h, dot_nn, dw)
    pl.semaphore_wait(barrier, 2 * HOP + n_voc - 1)
    ring_scatter("v", pv, pv_s, pv_r, pv_n, v_rows)
    remote(
        t_any.at[pl.ds(0, 8)], t.at[pl.ds(rows, 8)], "halo", ring_peer(-1)
    ).start()

    remote(pa.at[twin_half], pair_a, "pair_a", twin_id).start()
    half_dots(pa, core * half, h, dot_nn, dw)
    wait_for(pair_a, "pair_a")
    pa2[...] = (pa[mine_half, :] + pair_a[...]).astype(pa2.dtype)
    scatter(pa2, a_rows, rv_a, "rs_a", chip_peer, chip, chips)

    turn(h, h_t)
    loads[4].wait()
    loads[5].wait()
    ring_relay("v", pv, pv_o, pv_f, pv_r, v_rows)
    wait_for(t.at[pl.ds(rows, 8)], "halo")
    t[pl.ds(rows, 8), :] = jnp.where(g == n_grp - 1, 0.0, t[pl.ds(rows, 8), :])

    def target_pass(index):
        start = pl.multiple_of(index * CHUNK, CHUNK)
        at = pl.ds(start, CHUNK)
        block = t[pl.ds(start, CHUNK + 8), :]
        shifted = pltpu.roll(block, CHUNK + 8 - HEAD, 0)[:CHUNK]
        top = jnp.max(shifted, -1, keepdims=True)
        low = shifted - top
        expo = jnp.exp(low)
        ssh[at, :] = low
        et[at, :] = expo
        norm = jnp.sum(expo, -1, keepdims=True)
        lane = lax.broadcasted_iota(jnp.int32, (CHUNK, 128), 1)
        statcol[at, :] = jnp.where(lane == 0, top, jnp.where(lane == 1, norm, 0.0))
        ids = lab[:, at].astype(F32)
        which = lax.broadcasted_iota(jnp.int32, ids.shape, 0)
        label = jnp.sum(jnp.where(which == book, ids, 0.0), 0, keepdims=True)
        label = label - (part * width).astype(F32)
        labc[at, :] = jnp.broadcast_to(label, (CHUNK, CHUNK)).T
    loop(rows // CHUNK, target_pass)
    comb[...] = jnp.zeros_like(comb)

    ring_own = pl.ds(pl.multiple_of(g * v_rows, v_rows), v_rows)
    vp[ring_own, :] = ring_total("v", pv, pv_f, pv_n, v_rows).astype(BF16)
    ring_gather("v", vp, v_rows)

    a_start = chip * a_rows
    own_a = pl.ds(pl.multiple_of(a_start, a_rows), a_rows)
    wait_for(rv_a, "rs_a")
    pre_own = total(pa2[own_a, :].astype(F32), rv_a, chips)
    pre[...] = pre_own
    acts_at = core * half + a_start
    acts[pl.ds(pl.multiple_of(acts_at, a_rows), a_rows), :] = (
        pre_own / (1.0 + jnp.exp(-pre_own))
    ).astype(BF16)
    gather(acts, a_rows, acts_at, "ag_a", chip_peer, chips)
    ring_forward("v", vp, v_rows)

    wait_for(acts.at[pl.ds(0, (chips - 1) * a_rows)], "ag_a")
    remote(acts.at[mine_half], acts.at[mine_half], "back_a", twin_id).start()

    ring_done("v", vp, v_rows)

    def label_mask(at):
        labels = labc[at, :]
        col = lax.broadcasted_iota(jnp.int32, (CHUNK, 128), 1).astype(F32)
        return jnp.concatenate([labels == col + 128.0 * k for k in range(width // 128)], 1)

    def draft_pass(side, index):
        local = pl.ds(pl.multiple_of(index * CHUNK, CHUNK), CHUNK)
        at = pl.ds(pl.multiple_of(side * half + index * CHUNK, CHUNK), CHUNK)
        draft = t[at, :] + dot_nn(acts[at, :], vp[...])
        top = jnp.max(draft, -1, keepdims=True)
        low = draft - top
        expo = jnp.exp(low)
        ed[at, :] = expo
        norm = jnp.sum(expo, -1, keepdims=True)
        cross = jnp.sum(et[at, :] * (ssh[at, :] - low), -1, keepdims=True)
        picked = jnp.sum(jnp.where(label_mask(at), draft, 0.0), -1, keepdims=True)
        lane = lax.broadcasted_iota(jnp.int32, (CHUNK, 128), 1)
        cols = statcol[at, :]
        cols = jnp.where(lane == 2, top, cols)
        cols = jnp.where(lane == 3, norm, cols)
        cols = jnp.where(lane == 4, cross, cols)
        cols = jnp.where(lane == 5, picked, cols)
        stat[side, :, local] = cols.T[:8]
    wait_for(acts.at[twin_half], "back_a")
    steps = half // CHUNK
    for side in range(2):
        loop(steps, functools.partial(draft_pass, side))
        for offset in range(1, per_book):
            remote(
                stat.at[side], rv_s.at[side, offset - 1], f"s{side}{offset}", book_peer(offset)
            ).start()
    turn(acts, acts_t)

    def row(block, k):
        return block[k:k + 1, :]

    def combine(side):
        for offset in range(1, per_book):
            wait_for(rv_s.at[side, offset - 1], f"s{side}{offset}")
        blocks = [stat[side]] + [rv_s[side, k] for k in range(per_book - 1)]
        top_t = functools.reduce(jnp.maximum, [row(b, 0) for b in blocks])
        top_d = functools.reduce(jnp.maximum, [row(b, 2) for b in blocks])
        fac_t = [jnp.exp(row(b, 0) - top_t) for b in blocks]
        fac_d = [jnp.exp(row(b, 2) - top_d) for b in blocks]
        sum_t = sum(row(b, 1) * f for b, f in zip(blocks, fac_t))
        sum_d = sum(row(b, 3) * f for b, f in zip(blocks, fac_d))
        cross = sum(
            f * (row(b, 4) + row(b, 1) * ((row(b, 0) - top_t) - (row(b, 2) - top_d)))
            for b, f in zip(blocks, fac_t)
        )
        picked = sum(row(b, 5) for b in blocks) - top_d - jnp.log(sum_d)
        frame = g * rows + side * half + lax.broadcasted_iota(jnp.int32, (1, half), 1)
        live = (frame < rows * n_grp - HEAD).astype(F32)
        diverge = cross / sum_t - jnp.log(sum_t) + jnp.log(sum_d)
        at = pl.ds(side * half, half)
        comb[0:1, at] = (live + LAM) * fac_d[0] / sum_d
        comb[1:2, at] = live * fac_t[0] / sum_t
        comb[2:3, at] = live * diverge - LAM * picked

    def grad_pass(index):
        at = pl.ds(pl.multiple_of(index * CHUNK, CHUNK), CHUNK)
        cols = comb[:, at].T
        value = ed[at, :] * cols[:, 0:1] - et[at, :] * cols[:, 1:2]
        value = value - jnp.where(label_mask(at), LAM, 0.0)
        grad[at, :] = value.astype(BF16)
    for side in range(2):
        combine(side)
        loop(steps, lambda index: grad_pass(side * steps + index))
    block_rows = rows // per_book
    loss_ref[0] = comb[2:3, pl.ds(pl.multiple_of(part * block_rows, block_rows), block_rows)]

    half_dots(pb, other * half, grad, dot_nt, vp)
    remote(pb.at[twin_half], pair_b, "pair_b", twin_id).start()
    pp[...] = dot_nn(acts_t[...], grad[...])
    pp_s[...] = pp[...].astype(pp_s.dtype)
    ring_scatter("p", pp, pp_s, pp_r, pp_n, v_rows)

    half_dots(pb, core * half, grad, dot_nt, vp)
    wait_for(pair_b, "pair_b")
    pb2[...] = (pb[mine_half, :] + pair_b[...]).astype(pb2.dtype)
    scatter(pb2, a_rows, rv_b, "rs_b", chip_peer, chip, chips)
    ring_relay("p", pp, pp_o, pp_f, pp_r, v_rows)
    proj[ring_own, :] = ring_total("p", pp, pp_f, pp_n, v_rows).astype(BF16)
    ring_gather("p", proj, v_rows)
    wait_for(rv_b, "rs_b")
    act_grad = total(pb2[own_a, :].astype(F32), rv_b, chips)
    sigma = 1.0 / (1.0 + jnp.exp(-pre[...]))
    slope = sigma * (1.0 + pre[...] * (1.0 - sigma))
    pg[pl.ds(pl.multiple_of(acts_at, a_rows), a_rows), :] = (act_grad * slope).astype(BF16)
    gather(pg, a_rows, acts_at, "ag_b", chip_peer, chips)

    ring_forward("p", proj, v_rows)

    wait_for(pg.at[pl.ds(0, (chips - 1) * a_rows)], "ag_b")
    remote(pg.at[mine_half], pg.at[mine_half], "back_b", twin_id).start()
    px[...] = dot_nn(h_t[:, mine_half], pg[mine_half, :])
    wait_for(pg.at[twin_half], "back_b")
    px[...] = px[...] + dot_nn(h_t[:, twin_half], pg[twin_half, :])
    px_s[...] = px[...].astype(px_s.dtype)
    ring_scatter("g", px, px_s, px_r, px_n, v_rows)

    ring_done("p", proj, v_rows)
    up = dot_nt(proj[...], hw[...])
    for side in range(2):
        pc[side] = up[:, side * half_w:(side + 1) * half_w]
        pc_s[side] = up[:, side * half_w:(side + 1) * half_w].astype(pc_s.dtype)

    def c_block(ref, device):
        return ref.at[device % 2, pl.ds(pl.multiple_of(device // 2 * c_rows, c_rows), c_rows)]

    def send_c(index):
        offset = ordered(index, n_voc)
        target = lax.rem(v + offset, n_voc)
        remote(c_block(pc_s, target), rv_c.at[offset - 1], "rs_c", voc_peer(offset)).start()
    loop(n_voc - 1, send_c)

    ring_relay("g", px, px_o, px_f, px_r, v_rows)
    gag[ring_own, :] = ring_total("g", px, px_f, px_n, v_rows).astype(gag.dtype)
    ring_gather("g", gag, v_rows)

    wait_for(rv_c, "rs_c")
    c_block(gall, v)[...] = total(c_block(pc, v)[...], rv_c, n_voc).astype(gall.dtype)

    def share_c(index):
        block = c_block(gall, v)
        remote(block, block, "ag_c", voc_peer(ordered(index, n_voc))).start()
    loop(n_voc - 1, share_c)
    ring_forward("g", gag, v_rows)
    ring_done("g", gag, v_rows)
    ga_ref[...] = gag[...]
    wait_for(rv_c, "ag_c")
    gb_ref[...] = gall[...]

    wait_sent(t.at[pl.ds(rows, 8)], "halo")
    wait_sent(pair_a, "pair_a")
    wait_sent(rv_a, "rs_a")
    wait_sent(acts.at[pl.ds(0, (chips - 1) * a_rows)], "ag_a")
    wait_sent(acts.at[mine_half], "back_a")
    ring_sent("v", pv_f, pv_r, pv_n, vp, v_rows)
    for side in range(2):
        for offset in range(1, per_book):
            wait_sent(stat.at[side], f"s{side}{offset}")
    wait_sent(pair_b, "pair_b")
    wait_sent(rv_b, "rs_b")
    wait_sent(pg.at[pl.ds(0, (chips - 1) * a_rows)], "ag_b")
    wait_sent(pg.at[mine_half], "back_b")
    ring_sent("p", pp_f, pp_r, pp_n, proj, v_rows)
    ring_sent("g", px_f, px_r, px_n, gag, v_rows)
    wait_sent(rv_c, "rs_c")
    wait_sent(rv_c, "ag_c")


def finish(loss_ref, ga_ref, gb_ref, loss_out, ga_out, gb_out):
    half_w = gb_ref.shape[2]
    loss_out[...] = loss_ref[...]
    ga_out[...] = ga_ref[...].astype(F32)
    for side in range(2):
        gb_out[:, side * half_w:(side + 1) * half_w] = gb_ref[side].astype(F32)


def on_device(n_grp, n_voc, hidden_states, target_logits, labels, down_weight, up_weight, head_weight):
    rows, width = target_logits.shape
    n_book = labels.shape[1]
    per_book = n_voc // n_book
    deep = hidden_states.shape[1]
    rank = up_weight.shape[0]
    span = up_weight.shape[1]
    chips = n_voc // 2
    half = rows // 2
    a_rows = half // chips
    v_rows = rank // n_grp
    c_rows = rank // chips
    half_w = span // 2
    vm = pltpu.VMEM
    w = WIRE
    scratch = [
        vm((rows, deep), BF16), vm((rows + 8, width), F32), vm((n_book, rows), jnp.int32), vm((deep, rank), BF16),
        vm((rank, span), BF16), vm((span, width), BF16), vm((deep, rows), BF16),
        vm((rank, width), F32), vm((rank, width), w["v"]), vm((2, v_rows, width), w["vx"]),
        vm((2, v_rows, width), w["vx"]), vm((2 * HOP - 2, v_rows, width), w["vn"]),
        vm((2 * HOP - 1, v_rows, width), w["v"]), vm((rank, width), BF16),
        vm((rows, rank), F32), vm((half, rank), F32),
        vm((half, rank), w["a"]), vm((chips - 1, a_rows, rank), w["a"]), vm((a_rows, rank), F32),
        vm((rows, rank), BF16), vm((rank, rows), BF16),
        vm((rows, 128), F32), vm((rows, width), F32), vm((rows, width), F32),
        vm((rows, width), F32), vm((rows, 128), F32), vm((2, 8, half), F32),
        vm((2, per_book - 1, 8, half), F32), vm((128, rows), F32), vm((rows, width), BF16),
        vm((rank, width), F32), vm((rank, width), w["p"]), vm((2, v_rows, width), w["px"]),
        vm((2, v_rows, width), w["px"]), vm((2 * HOP - 2, v_rows, width), w["pn"]),
        vm((2 * HOP - 1, v_rows, width), w["p"]), vm((rank, width), BF16),
        vm((rows, rank), F32), vm((half, rank), F32),
        vm((half, rank), w["b"]), vm((chips - 1, a_rows, rank), w["b"]), vm((rows, rank), BF16),
        vm((deep, rank), F32), vm((deep, rank), w["g"]), vm((2, v_rows, rank), w["gx"]),
        vm((2, v_rows, rank), w["gx"]), vm((2 * HOP - 2, v_rows, rank), w["gn"]),
        vm((2 * HOP - 1, v_rows, rank), w["g"]), vm((deep, rank), w["ga"]),
        vm((2, rank, half_w), F32), vm((2, rank, half_w), w["c"]),
        vm((n_voc - 1, c_rows, half_w), w["c"]), vm((2, rank, half_w), w["c"]),
        pltpu.SemaphoreType.DMA((6,)),
        pltpu.SemaphoreType.DMA((len(PHASES),)),
        pltpu.SemaphoreType.DMA((len(PHASES),)),
    ]
    hbm = pl.BlockSpec(memory_space=pl.ANY)
    vmem = pl.BlockSpec(memory_space=pltpu.VMEM)
    parts = pl.pallas_call(
        functools.partial(kernel, n_grp, n_voc, n_book),
        out_shape=(
            vm((1, 1, rows // per_book), F32),
            vm((deep, rank), w["ga"]),
            vm((2, rank, half_w), w["c"]),
        ),
        in_specs=[hbm] * 6,
        out_specs=(vmem, vmem, vmem),
        scratch_shapes=scratch,
        compiler_params=pltpu.CompilerParams(
            collective_id=0, has_side_effects=True, vmem_limit_bytes=56 * 1024 * 1024
        ),
    )(hidden_states, target_logits, labels.T, down_weight, up_weight, head_weight)
    return pl.pallas_call(
        finish,
        out_shape=(
            jax.ShapeDtypeStruct((1, 1, rows // per_book), F32),
            jax.ShapeDtypeStruct((deep, rank), F32),
            jax.ShapeDtypeStruct((rank, span), F32),
        ),
        in_specs=[vmem] * 3,
        out_specs=(vmem, vmem, vmem),
        compiler_params=pltpu.CompilerParams(vmem_limit_bytes=4 * 1024 * 1024),
    )(*[pltpu.with_memory_space_constraint(part, pltpu.VMEM) for part in parts])


def solution(mesh):
    in_specs = (
        P("grp", "voc"),
        P("grp", "voc"),
        P("grp", None),
        P("voc", None),
        P(None, "grp"),
        P("grp", "voc"),
    )
    out_specs = (P("voc", "grp", None), P("voc", None), P(None, "grp"))
    return jax.shard_map(
        functools.partial(on_device, mesh.shape["grp"], mesh.shape["voc"]),
        mesh=mesh, in_specs=in_specs, out_specs=out_specs, check_vma=False,
    )
```
